32 devices in a mesh: wide: 8 (over y, x, core), narrow: 4 (over z).
Axes of the slice: x: 2, y: 2, z: 4, core: 2. Of those that a mesh axis runs over, the one named last changes fastest.
Arguments:
- tokens: bfloat16 [16384, 768], P(('wide', 'narrow')), may hold values from -6 to 6
- noise: int32 [16384], P(('wide', 'narrow')), may hold values 0 or 1
- seq_lengths: int32 [8, 4], P('wide'), may hold values from 0 to 2048, as said below
- ln1_gain: float32 [768], replicated, may hold values from 0.25 to 1.75
- ln1_bias: float32 [768], replicated, may hold values from -3 to 3
- qkv_weight: bfloat16 [3, 768, 768], P(None, None, 'narrow'), may hold values from -0.21875 to 0.21875
- out_weight: bfloat16 [768, 768], P('narrow'), may hold values from -3 to 3
- ln2_gain: float32 [768], replicated, may hold values from 0.25 to 1.75
- ln2_bias: float32 [768], replicated, may hold values from -3 to 3
- up_weight: bfloat16 [768, 3072], P(None, 'narrow'), may hold values from -0.21875 to 0.21875
- up_bias: float32 [3072], P('narrow'), may hold values from -4 to 4
- down_weight: bfloat16 [3072, 768], P('narrow'), may hold values from -0.109375 to 0.109375
- down_bias: float32 [768], replicated, may hold values from -3 to 3
- mask_vector: float32 [768], replicated, may hold values from -4 to 4
- cotangent: bfloat16 [2, 16384, 768], P(None, ('wide', 'narrow')), may hold values from -6 to 6
Outputs:
- output: bfloat16 [2, 16384, 768], P(None, ('wide', 'narrow'))
- d_tokens: bfloat16 [16384, 768], P(('wide', 'narrow'))
- d_ln1_gain: float32 [768], replicated
- d_ln1_bias: float32 [768], replicated
- d_qkv_weight: float32 [3, 768, 768], P(None, 'wide', 'narrow')
- d_out_weight: float32 [768, 768], P('narrow', 'wide')
- d_ln2_gain: float32 [768], replicated
- d_ln2_bias: float32 [768], replicated
- d_up_weight: float32 [768, 3072], P('wide', 'narrow')
- d_up_bias: float32 [3072], P(('narrow', 'wide'))
- d_down_weight: float32 [3072, 768], P('narrow', 'wide')
- d_down_bias: float32 [768], replicated
- d_mask_vector: float32 [768], replicated
The draws below stay inside these ranges and needn't reach their ends.
Inputs may be any that keep to these rules, and one draw needn't show every extreme that they name: `seq_lengths`: row w lists the sequences packed on index w of wide in order; every length is a multiple of 16 and a row sums to 2048. A quarter of the rows hold one sequence of 2048 tokens followed by zeros; the others hold four sequences, each at least 1 token long.
All inputs are finite; a program needn't handle non-finite values. No bound on the sum of `noise` on one device may be relied on, other than what follows from the above.
Results may differ from the reference program's by a relative error of at most 0.019.
Values may be sent and summed in bfloat16 or wider, within the bound.
No kernel may reach another device: no remote copies, remote signals or barrier semaphores. Data moves between devices by JAX's collectives and lax.ppermute only.
A program may use at most 256 MiB of HBM per device.

```python
import math
import jax
import jax.numpy as jnp
from jax import lax

D = 768
HEADS = 12
HEAD = 64
FF = 3072
BLOCK = 16
G = 2048
SLOTS = 4
GROUPS = 8
TOKENS = 16384


def draw_seq_lengths(key, part):
    long_key = jax.random.fold_in(key, 11)
    short_key = jax.random.fold_in(key, 23)
    order = jax.random.permutation(long_key, GROUPS)
    is_long = order < max(GROUPS // 4, 1)
    blocks = G // BLOCK
    spread = blocks // 8
    shifts = jax.random.randint(short_key, (GROUPS, 2), -spread, spread + 1).astype(jnp.int32)
    first = blocks // 4 + shifts[:, 0]
    third = blocks // 4 + shifts[:, 1]
    short = jnp.stack([first, blocks // 2 - first, third, blocks // 2 - third], axis=1) * BLOCK
    long_row = jnp.concatenate([jnp.full((GROUPS, 1), G, dtype=jnp.int32), jnp.zeros((GROUPS, SLOTS - 1), dtype=jnp.int32)], axis=1)
    return jnp.where(is_long[:, None], long_row, short.astype(jnp.int32)).astype(jnp.int32)


def place_ends(entries, rng, smallest, top_value):
    shape = entries.shape
    index_at = [jax.random.randint(jax.random.fold_in(rng, axis), (), 0, shape[axis]) for axis in range(len(shape))]
    entries = entries.at[tuple(index_at)].set(smallest)
    longest = shape.index(max(shape))
    index_at[longest] = (index_at[longest] + 1) % shape[longest]
    return entries.at[tuple(index_at)].set(top_value)


def spiked(values, key, source, target, parts, factor):
    owner, partner = [(jnp.arange(values.shape[position]) // (values.shape[position] // parts)).reshape([-1 if axis == position else 1 for axis in range(values.ndim)]) for position in (source, target)]
    chosen = jax.random.permutation(key, parts)[partner]
    strong = (owner == chosen) | (owner == (partner + parts // 2) % parts)
    return jnp.where(strong, factor * values, values)


def level_of(own_key, shape, split, least, top_value):
    factor_of = 1.0
    for position, parts in split:
        steps = jax.random.uniform(jax.random.fold_in(jax.random.fold_in(own_key, 6), position), (parts,), jnp.float32, least / len(split), top_value / len(split))
        factor_of = factor_of * jnp.repeat(jnp.exp(steps), shape[position] // parts).reshape((-1,) + (1,) * (len(shape) - 1 - position))
    return factor_of


def centred(rng, shape, scale, most, cuts=(), kind=jnp.bfloat16):
    entries = jax.random.normal(rng, shape, jnp.float32) * scale
    if len(cuts) > 0:
        entries = level_of(rng, shape, cuts, -0.22, 0.18) * entries
    return jnp.clip(entries, min=-most, max=most).astype(kind)


def noise_with(own_key, dims, deviation, limit, shards, heavy, kind=jnp.bfloat16):
    values = deviation * jax.random.normal(own_key, dims, jnp.float32)
    if shards:
        values = values * level_of(own_key, dims, shards, -0.22, 0.18)
    return jnp.clip(spiked(values, jax.random.fold_in(own_key, 3), *heavy), -limit, limit).astype(kind)


def setup_inputs(seed: int = 0) -> dict:
    splits = jax.random.split(jax.random.key(seed), 16)
    return {
        "tokens": noise_with(splits[0], (TOKENS, D), 1.0, 6.0, ((0, 32),), (0, 1, 32, 2.75)),
        "noise": place_ends((jax.random.randint(splits[1], (TOKENS,), 0, 2) < 1).astype(jnp.int32), jax.random.fold_in(splits[1], 1), 0, 1),
        "seq_lengths": draw_seq_lengths(jax.random.fold_in(splits[15], 71), 0),
        "ln1_gain": jnp.clip(1.0 + 0.15 * jax.random.normal(splits[3], (D,), jnp.float32), 0.25, 1.75),
        "ln1_bias": centred(splits[4], (D,), 0.5, 3.0, (), jnp.float32),
        "qkv_weight": centred(splits[5], (3, D, D), D ** -0.5, 0.21875, ((2, 4),)),
        "out_weight": centred(splits[6], (D, D), 4 ** -0.5, 3.0, ((0, 4),)),
        "ln2_gain": jnp.clip(1.0 + 0.15 * jax.random.normal(splits[7], (D,), jnp.float32), 0.25, 1.75),
        "ln2_bias": centred(splits[8], (D,), 0.5, 3.0, (), jnp.float32),
        "up_weight": centred(splits[9], (D, FF), D ** -0.5, 0.21875, ((1, 4),)),
        "up_bias": centred(splits[10], (FF,), 1.0, 4.0, ((0, 4),), jnp.float32),
        "down_weight": centred(splits[11], (FF, D), FF ** -0.5, 0.109375, ((0, 4),)),
        "down_bias": centred(splits[12], (D,), 0.5, 3.0, (), jnp.float32),
        "mask_vector": centred(splits[13], (D,), 1.0, 4.0, (), jnp.float32),
        "cotangent": noise_with(splits[14], (2, TOKENS, D), 1.0, 6.0, ((1, 32),), (1, 2, 32, 2.75)),
    }


@jax.custom_vjp
def low(v):
    return lax.optimization_barrier(v.astype(jnp.bfloat16)).astype(jnp.float32)

@jax.custom_vjp
def low_back(v):
    return v

def low_keep(v):
    return (low(v), None)

def low_pass(kept, grad):
    return (grad,)

def back_keep(v):
    return (v, None)

def back_low(kept, grad):
    return (low(grad),)
low.defvjp(low_keep, low_pass)
low_back.defvjp(back_keep, back_low)
EPS = 1e-05
HIGH = lax.Precision.HIGHEST

def layer_norm(values, gain, shift):
    center = values - lax.optimization_barrier(jnp.mean(values, axis=-1, keepdims=True))
    spread = lax.optimization_barrier(jnp.mean(center * center, axis=-1, keepdims=True))
    return center * lax.rsqrt(spread + EPS) * gain + shift

def gelu_tanh(values):
    return jax.nn.gelu(values, approximate=True)

def rotate(values, cosines, sines):
    half = values.shape[-1] // 2
    turned = jnp.concatenate([-values[..., half:], values[..., :half]], axis=-1)
    return values * cosines + turned * sines

def angle_tables(positions, head):
    index_f = jnp.arange(head // 2).astype(jnp.float32)
    freqs = jnp.exp(index_f * (-2.0 * math.log(10000.0) / head))
    angles = positions.astype(jnp.float32)[:, None] * freqs[None, :]
    cosines = jnp.concatenate([jnp.cos(angles), jnp.cos(angles)], axis=-1)[:, None, :]
    sines = jnp.concatenate([jnp.sin(angles), jnp.sin(angles)], axis=-1)[:, None, :]
    return (cosines, sines)

def token_meta(lengths_row, count, block):
    lengths_row = lengths_row.astype(jnp.int32)
    ends = jnp.cumsum(lengths_row).astype(jnp.int32)
    starts = (ends - lengths_row).astype(jnp.int32)
    places = jnp.arange(count).astype(jnp.int32)
    seq_id = lax.optimization_barrier(jnp.sum((places[:, None] >= ends[None, :]).astype(jnp.int32), axis=1)).astype(jnp.int32)
    slot_ids = jnp.arange(lengths_row.shape[0]).astype(jnp.int32)
    first = lax.optimization_barrier(jnp.sum(jnp.where(seq_id[:, None] == slot_ids[None, :], starts[None, :], 0), axis=1)).astype(jnp.int32)
    return (seq_id, (places - first).astype(jnp.int32), (places // block).astype(jnp.int32))

def allowed_pairs(q_seq, q_blk, q_copy, k_seq, k_blk, k_copy):
    same = q_seq[:, None] == k_seq[None, :]
    q_b = q_blk[:, None]
    k_b = k_blk[None, :]
    q_noisy = q_copy[:, None] == 0
    k_noisy = k_copy[None, :] == 0
    rule = jnp.where(q_noisy, jnp.where(k_noisy, q_b == k_b, k_b < q_b), jnp.logical_and(jnp.logical_not(k_noisy), k_b <= q_b))
    return jnp.logical_and(same, rule)

def group_forward(params, x_group, noise_group, seq2, pos2, blk2, copy2):
    ln1_gain, ln1_bias, qkv_weight, out_weight, ln2_gain, ln2_bias, up_weight, up_bias, down_weight, down_bias, mask_vector = params
    count = 2 * x_group.shape[0]
    noisy = jnp.where(noise_group[:, None] == 1, mask_vector[None, :], x_group)
    resid = jnp.concatenate([noisy, x_group], axis=0)
    normed = low(layer_norm(resid, ln1_gain, ln1_bias))
    cosines, sines = angle_tables(pos2, HEAD)
    q_pre = low_back(jnp.dot(normed, qkv_weight[0], precision=HIGH)).reshape(count, HEADS, HEAD)
    k_pre = low_back(jnp.dot(normed, qkv_weight[1], precision=HIGH)).reshape(count, HEADS, HEAD)
    queries = low(rotate(q_pre, cosines, sines))
    keys = low(rotate(k_pre, cosines, sines))
    values = low(low_back(jnp.dot(normed, qkv_weight[2], precision=HIGH))).reshape(count, HEADS, HEAD)
    width_q = min(512, count)
    count_b = count // width_q
    scale = 1.0 / math.sqrt(HEAD)

    def attend(item):
        q_block, q_seq, q_blk, q_copy = item
        scores = low_back(jnp.einsum('qhd,khd->hqk', q_block, keys, precision=HIGH) * scale)
        mask = allowed_pairs(q_seq, q_blk, q_copy, seq2, blk2, copy2)
        scores = jnp.where(mask[None], scores, -1e+30)
        top = lax.optimization_barrier(jnp.max(scores, axis=2, keepdims=True))
        lse = top + jnp.log(lax.optimization_barrier(jnp.sum(jnp.exp(scores - top), axis=2, keepdims=True)))
        probs = low(jnp.exp(scores - lse))
        return jnp.einsum('hqk,khd->qhd', probs, values, precision=HIGH)
    blocks_out = lax.map(jax.checkpoint(attend), (queries.reshape(count_b, width_q, HEADS, HEAD), seq2.reshape(count_b, width_q), blk2.reshape(count_b, width_q), copy2.reshape(count_b, width_q)))
    attn = low(low_back(blocks_out.reshape(count, HEADS * HEAD)))
    h_mid = resid + low_back(jnp.dot(attn, out_weight, precision=HIGH))
    normed2 = low(layer_norm(h_mid, ln2_gain, ln2_bias))
    up_pre = low_back(jnp.dot(normed2, up_weight, precision=HIGH) + up_bias)
    hidden = low(gelu_tanh(up_pre))
    return h_mid + low_back(jnp.dot(hidden, down_weight, precision=HIGH)) + down_bias

def reference(tokens, noise, seq_lengths, ln1_gain, ln1_bias, qkv_weight, out_weight, ln2_gain, ln2_bias, up_weight, up_bias, down_weight, down_bias, mask_vector, cotangent):
    params = tuple((p.astype(jnp.float32) for p in (ln1_gain, ln1_bias, qkv_weight, out_weight, ln2_gain, ln2_bias, up_weight, up_bias, down_weight, down_bias, mask_vector)))
    width = tokens.shape[1]
    x_all = tokens.astype(jnp.float32).reshape(GROUPS, G, width)
    noise_all = noise.reshape(GROUPS, G)
    cot_all = cotangent.astype(jnp.float32).reshape(2, GROUPS, G, width).transpose(1, 0, 2, 3)

    def step(totals, item):
        x_group, noise_group, lengths_row, cot_group = item
        seq_id, pos, blk = token_meta(lengths_row, G, BLOCK)
        seq2 = jnp.concatenate([seq_id, seq_id])
        pos2 = jnp.concatenate([pos, pos])
        blk2 = jnp.concatenate([blk, blk])
        copy2 = jnp.concatenate([jnp.zeros((G,), jnp.int32), jnp.ones((G,), jnp.int32)])

        def forward(prm, xg):
            return group_forward(prm, xg, noise_group, seq2, pos2, blk2, copy2)
        result, pull = jax.vjp(forward, params, x_group)
        d_params, d_x = pull(cot_group.reshape(2 * G, width))
        totals = jax.tree.map(lambda left, right: left + right, totals, d_params)
        return (totals, (result.reshape(2, G, width), d_x))
    zeros = tuple((jnp.zeros_like(p) for p in params))
    totals, (results, d_xs) = lax.scan(step, zeros, (x_all, noise_all, seq_lengths, cot_all))
    output = results.transpose(1, 0, 2, 3).reshape(2, TOKENS, width).astype(jnp.bfloat16)
    d_tokens = d_xs.reshape(TOKENS, width).astype(jnp.bfloat16)
    return (output, d_tokens, totals[0], totals[1], totals[2], totals[3], totals[4], totals[5], totals[6], totals[7], totals[8], totals[9], totals[10])
```

```python
import math

import jax
import jax.numpy as jnp
from jax import lax
from jax.experimental import pallas as pl
from jax.experimental.pallas import tpu as pltpu
from jax.sharding import PartitionSpec as P

HEAD = 64
BLOCK = 16
EPS = 1e-05


TILE = 256
NEG = -1e30


def nt(left, right):
    return lax.dot_general(
        left, right, (((1,), (1,)), ((), ())), preferred_element_type=jnp.float32
    )


def nn(left, right):
    return lax.dot_general(
        left, right, (((1,), (0,)), ((), ())), preferred_element_type=jnp.float32
    )


def project_kernel(a, amask, masked, w, wrot, cosines, sines, q, k, kt, v, vt):
    rows = a[...]
    spot = amask[...]
    cos = cosines[...]
    sin = sines[...]
    hidden = jnp.broadcast_to(masked[...], cos.shape) == 1
    heads = q.shape[0]

    def both(index, turned):
        pre = nn(rows, w[index])
        pre_m = nn(spot, w[index])[0:1]
        noisy = jnp.where(hidden, pre_m, pre)
        if not turned:
            return noisy, pre
        side = nn(rows, wrot[index])
        side_m = nn(spot, wrot[index])[0:1]
        side_n = jnp.where(hidden, side_m, side)
        return noisy * cos + side_n * sin, pre * cos + side * sin

    for index, (flat, trans) in enumerate(((q, None), (k, kt), (v, vt))):
        pair = both(index, index < 2)
        for copy in range(2):
            low = pair[copy].astype(jnp.bfloat16)
            if index == 0:
                low = low * jnp.asarray(1.0 / math.sqrt(HEAD), jnp.bfloat16)
            for head in range(heads):
                piece = low[:, head * HEAD : (head + 1) * HEAD]
                flat[head, copy] = piece
                if trans is not None:
                    trans[head, copy] = piece.T


def tile_masks(start, base, tile):
    key = lax.broadcasted_iota(jnp.int32, (tile, tile), 0)
    query = lax.broadcasted_iota(jnp.int32, (tile, tile), 1)
    kb = key // BLOCK
    qb = query // BLOCK
    same = key + base >= start
    return kb == qb, jnp.logical_and(kb < qb, same), jnp.logical_and(kb <= qb, same)


def forward_kernel(span, q, kn, kc, vtn, vtc, start, attn, lse):
    i = pl.program_id(0)
    heads = q.shape[0]
    tile = q.shape[2]
    base = i * tile
    starts = start[...]
    own, below, upto = tile_masks(starts, base, tile)
    starts2 = jnp.concatenate([starts, starts], axis=1)
    queries = [q[h].reshape(2 * tile, HEAD) for h in range(heads)]
    tops, sums, accs = [], [], []
    at = pl.ds(base, tile)
    for h in range(heads):
        s0 = jnp.where(own, nt(kn[h, 0], queries[h][:tile]), NEG)
        sd = nt(kc[h, 0, at, :], queries[h])
        s1 = jnp.where(below, sd[:, :tile], NEG)
        s2 = jnp.where(upto, sd[:, tile:], NEG)
        top_n = jnp.maximum(
            jnp.max(s0, axis=0, keepdims=True), jnp.max(s1, axis=0, keepdims=True)
        )
        top_c = jnp.max(s2, axis=0, keepdims=True)
        p0 = jnp.exp(s0 - top_n)
        p1 = jnp.exp(s1 - top_n)
        p2 = jnp.exp(s2 - top_c)
        sum_n = jnp.sum(p0, axis=0, keepdims=True) + jnp.sum(p1, axis=0, keepdims=True)
        sum_c = jnp.sum(p2, axis=0, keepdims=True)
        values = vtc[h, 0, :, at]
        acc_n = nn(vtn[h, 0], p0.astype(jnp.bfloat16)) + nn(values, p1.astype(jnp.bfloat16))
        acc_c = nn(values, p2.astype(jnp.bfloat16))
        tops.append(jnp.concatenate([top_n, top_c], axis=1))
        sums.append(jnp.concatenate([sum_n, sum_c], axis=1))
        accs.append(jnp.concatenate([acc_n, acc_c], axis=1))

    def step(masked):
        def body(j, carry):
            tops, sums, accs = carry
            here = pl.ds(pl.multiple_of(j * tile, tile), tile)
            out_t, out_s, out_a = [], [], []
            for h in range(heads):
                s = nt(kc[h, 0, here, :], queries[h])
                if masked:
                    key = lax.broadcasted_iota(jnp.int32, s.shape, 0) + j * tile
                    s = jnp.where(key >= starts2, s, NEG)
                top = jnp.maximum(tops[h], jnp.max(s, axis=0, keepdims=True))
                keep = jnp.exp(tops[h] - top)
                p = jnp.exp(s - top)
                out_t.append(top)
                out_s.append(sums[h] * keep + jnp.sum(p, axis=0, keepdims=True))
                out_a.append(accs[h] * keep + nn(vtc[h, 0, :, here], p.astype(jnp.bfloat16)))
            return out_t, out_s, out_a

        return body

    carry = lax.fori_loop(span[0, i], span[1, i], step(True), (tops, sums, accs))
    tops, sums, accs = lax.fori_loop(span[1, i], i, step(False), carry)
    outs = []
    for h in range(heads):
        outs.append((accs[h] * (1.0 / sums[h])).T)
        row = tops[h] + jnp.log(sums[h])
        lse[2 * h : 2 * h + 1, :] = row[:, :tile]
        lse[2 * h + 1 : 2 * h + 2, :] = row[:, tile:]
    merged = jnp.concatenate(outs, axis=1).astype(jnp.bfloat16)
    attn[0] = merged[:tile]
    attn[1] = merged[tile:]


def unturn(values, cos, sin):
    w = values * sin
    parts = []
    for h in range(values.shape[1] // HEAD):
        lo = h * HEAD
        mid = lo + HEAD // 2
        parts += [w[:, mid : lo + HEAD], -w[:, lo:mid]]
    return values * cos + jnp.concatenate(parts, axis=1)


def backward_kernel(
    span, q, kn, kc, ktn, ktc, vn, vc, grad, attn, lse, start, masked, cosines, sines, w,
    d_all, d_a, d_spot, dk_acc, dv_acc,
):
    p = pl.program_id(0)
    i = pl.num_programs(0) - 1 - p
    heads = q.shape[0]
    tile = q.shape[2]
    base = i * tile
    at = pl.ds(base, tile)

    @pl.when(p == 0)
    def _():
        dk_acc[...] = jnp.zeros_like(dk_acc)
        dv_acc[...] = jnp.zeros_like(dv_acc)
        d_spot[...] = jnp.zeros_like(d_spot)

    starts = start[...]
    own, below, upto = tile_masks(starts, base, tile)
    starts2 = jnp.concatenate([starts, starts], axis=1)
    queries, grads, lses, deltas = [], [], [], []
    grad_n, grad_c = grad[0], grad[1]
    dots_n = grad_n.astype(jnp.float32) * attn[0].astype(jnp.float32)
    dots_c = grad_c.astype(jnp.float32) * attn[1].astype(jnp.float32)
    for h in range(heads):
        lanes = slice(h * HEAD, (h + 1) * HEAD)
        queries.append(q[h].reshape(2 * tile, HEAD))
        grads.append(jnp.concatenate([grad_n[:, lanes], grad_c[:, lanes]], axis=0))
        lses.append(
            jnp.concatenate([lse[2 * h : 2 * h + 1, :], lse[2 * h + 1 : 2 * h + 2, :]], axis=1)
        )
        dots = jnp.concatenate([dots_n[:, lanes], dots_c[:, lanes]], axis=0)
        deltas.append(jnp.sum(dots.T, axis=0, keepdims=True))

    dqs, dk_noisy, dv_noisy = [], [], []
    for h in range(heads):
        qn, gn = queries[h][:tile], grads[h][:tile]
        s0 = nt(kn[h, 0], qn)
        p0 = jnp.where(own, jnp.exp(s0 - lses[h][:, :tile]), 0.0)
        ds0 = (p0 * (nt(vn[h, 0], gn) - deltas[h][:, :tile])).astype(jnp.bfloat16)
        dv_noisy.append(nn(p0.astype(jnp.bfloat16), gn))
        dk_noisy.append(nn(ds0, qn))
        dq_n = nn(ktn[h, 0], ds0)
        both = jnp.concatenate([below, upto], axis=1)
        s = nt(kc[h, 0, at, :], queries[h])
        pr = jnp.where(both, jnp.exp(jnp.where(both, s, NEG) - lses[h]), 0.0)
        ds = (pr * (nt(vc[h, 0, at, :], grads[h]) - deltas[h])).astype(jnp.bfloat16)
        dv_acc[h, at, :] += nn(pr.astype(jnp.bfloat16), grads[h])
        dk_acc[h, at, :] += nn(ds, queries[h])
        dq = nn(ktc[h, 0, :, at], ds)
        dqs.append(dq + jnp.concatenate([dq_n, jnp.zeros_like(dq_n)], axis=1))

    def step(masked_step):
        def body(j, carry):
            out = []
            here = pl.ds(pl.multiple_of(j * tile, tile), tile)
            for h in range(heads):
                s = nt(kc[h, 0, here, :], queries[h])
                if masked_step:
                    key = lax.broadcasted_iota(jnp.int32, s.shape, 0) + j * tile
                    s = jnp.where(key >= starts2, s, NEG)
                pr = jnp.exp(s - lses[h])
                ds = (pr * (nt(vc[h, 0, here, :], grads[h]) - deltas[h])).astype(jnp.bfloat16)
                dv_acc[h, here, :] += nn(pr.astype(jnp.bfloat16), grads[h])
                dk_acc[h, here, :] += nn(ds, queries[h])
                out.append(carry[h] + nn(ktc[h, 0, :, here], ds))
            return out

        return body

    carry = lax.fori_loop(span[0, i], span[1, i], step(True), dqs)
    dqs = lax.fori_loop(span[1, i], i, step(False), carry)

    scale = 1.0 / math.sqrt(HEAD)
    dq_n = jnp.concatenate([dqs[h][:, :tile].T for h in range(heads)], axis=1) * scale
    dq_c = jnp.concatenate([dqs[h][:, tile:].T for h in range(heads)], axis=1) * scale
    dk_c = jnp.concatenate([dk_acc[h, at, :] for h in range(heads)], axis=1)
    dv_c = jnp.concatenate([dv_acc[h, at, :] for h in range(heads)], axis=1)
    dk_n = jnp.concatenate(dk_noisy, axis=1)
    dv_n = jnp.concatenate(dv_noisy, axis=1)
    hidden = masked[...].astype(jnp.float32)
    shown = 1.0 - hidden
    cos, sin = cosines[...], sines[...]
    back = jnp.zeros(d_a.shape, jnp.float32)
    for index, (noisy, clean) in enumerate(((dq_n, dq_c), (dk_n, dk_c), (dv_n, dv_c))):
        kept = clean + shown * noisy
        gone = hidden * noisy
        if index < 2:
            kept = unturn(kept, cos, sin)
            gone = unturn(gone, cos, sin)
        low = kept.astype(jnp.bfloat16)
        d_all[index] = low
        back = back + nt(low, w[index])
        d_spot[index] += jnp.sum(gone.reshape(tile // 8, 8, gone.shape[1]), axis=0)
    d_a[...] = back.astype(jnp.bfloat16)


def tile_of(shape, axis, tile, turn):
    block = tuple(tile if d == axis else s for d, s in enumerate(shape))
    return pl.BlockSpec(block, lambda i, *_: tuple(turn(i) if d == axis else 0 for d in range(len(shape))))


def whole(shape):
    return pl.BlockSpec(shape, lambda i, *_: (0,) * len(shape))


def half(shape, copy, axis, tile, turn):
    block = tuple(1 if d == 1 else tile if d == axis else s for d, s in enumerate(shape))
    return pl.BlockSpec(
        block, lambda i, *_: tuple(copy if d == 1 else turn(i) if d == axis else 0 for d in range(len(shape)))
    )


def project(a, amask, masked, w, wrot, cosines, sines):
    group, width = a.shape
    lw = w.shape[2]
    heads = lw // HEAD
    tile = min(TILE, group)
    same = lambda i: i
    flat = (heads, 2, group, HEAD)
    trans = (heads, 2, HEAD, group)
    bf = jnp.bfloat16
    return pl.pallas_call(
        project_kernel,
        grid=(group // tile,),
        in_specs=[
            tile_of((group, width), 0, tile, same),
            whole(amask.shape),
            tile_of((group, 1), 0, tile, same),
            whole(w.shape),
            whole(wrot.shape),
            tile_of((group, lw), 0, tile, same),
            tile_of((group, lw), 0, tile, same),
        ],
        out_specs=[
            tile_of(flat, 2, tile, same),
            tile_of(flat, 2, tile, same),
            tile_of(trans, 3, tile, same),
            tile_of(flat, 2, tile, same),
            tile_of(trans, 3, tile, same),
        ],
        out_shape=[jax.ShapeDtypeStruct(s, bf) for s in (flat, flat, trans, flat, trans)],
        name="project",
    )(a, amask, masked, w, wrot, cosines, sines)


def attend(span, q, k, v_t, start):
    heads, _, group, _ = q.shape
    tile = min(TILE, group)
    same = lambda i: i
    lw = heads * HEAD
    return pl.pallas_call(
        forward_kernel,
        grid_spec=pltpu.PrefetchScalarGridSpec(
            num_scalar_prefetch=1,
            grid=(group // tile,),
            in_specs=[
                tile_of(q.shape, 2, tile, same),
                half(k.shape, 0, 2, tile, same),
                half(k.shape, 1, None, tile, same),
                half(v_t.shape, 0, 3, tile, same),
                half(v_t.shape, 1, None, tile, same),
                tile_of((1, group), 1, tile, same),
            ],
            out_specs=[
                tile_of((2, group, lw), 1, tile, same),
                tile_of((8, group), 1, tile, same),
            ],
        ),
        out_shape=[
            jax.ShapeDtypeStruct((2, group, lw), jnp.bfloat16),
            jax.ShapeDtypeStruct((8, group), jnp.float32),
        ],
        name="attend",
    )(span, q, k, k, v_t, v_t, start)


def attend_back(span, q, k, k_t, v, grad, attn, lse, start, masked, cosines, sines, w):
    heads, _, group, _ = q.shape
    tile = min(TILE, group)
    lw = heads * HEAD
    width = w.shape[1]
    last = group // tile - 1
    turn = lambda i: last - i
    return pl.pallas_call(
        backward_kernel,
        grid_spec=pltpu.PrefetchScalarGridSpec(
            num_scalar_prefetch=1,
            grid=(group // tile,),
            in_specs=[
                tile_of(q.shape, 2, tile, turn),
                half(k.shape, 0, 2, tile, turn),
                half(k.shape, 1, None, tile, turn),
                half(k_t.shape, 0, 3, tile, turn),
                half(k_t.shape, 1, None, tile, turn),
                half(v.shape, 0, 2, tile, turn),
                half(v.shape, 1, None, tile, turn),
                tile_of((2, group, lw), 1, tile, turn),
                tile_of((2, group, lw), 1, tile, turn),
                tile_of((8, group), 1, tile, turn),
                tile_of((1, group), 1, tile, turn),
                tile_of((group, 1), 0, tile, turn),
                tile_of((group, lw), 0, tile, turn),
                tile_of((group, lw), 0, tile, turn),
                whole(w.shape),
            ],
            out_specs=[
                tile_of((3, group, lw), 1, tile, turn),
                tile_of((group, width), 0, tile, turn),
                whole((3, 8, lw)),
            ],
            scratch_shapes=[
                pltpu.VMEM((heads, group, HEAD), jnp.float32),
                pltpu.VMEM((heads, group, HEAD), jnp.float32),
            ],
        ),
        out_shape=[
            jax.ShapeDtypeStruct((3, group, lw), jnp.bfloat16),
            jax.ShapeDtypeStruct((group, width), jnp.bfloat16),
            jax.ShapeDtypeStruct((3, 8, lw), jnp.float32),
        ],
        name="attend_back",
    )(span, q, k, k, k_t, k_t, v, v, grad, attn, lse, start, masked, cosines, sines, w)


def layer_norm(values, gain, shift):
    center = values - jnp.mean(values, axis=-1, keepdims=True)
    spread = jnp.mean(center * center, axis=-1, keepdims=True)
    return center * lax.rsqrt(spread + EPS) * gain + shift


def gelu_tanh(values):
    return jax.nn.gelu(values, approximate=True)


def token_meta(lengths_row, count):
    ends = jnp.cumsum(lengths_row)
    starts = ends - lengths_row
    places = jnp.arange(count)
    seq_id = jnp.sum((places[:, None] >= ends[None, :]).astype(jnp.int32), axis=1)
    slot_ids = jnp.arange(lengths_row.shape[0])
    first = jnp.sum(jnp.where(seq_id[:, None] == slot_ids[None, :], starts[None, :], 0), axis=1)
    return (first, places - first)


def angle_tables(positions, heads):
    index_f = jnp.arange(HEAD // 2).astype(jnp.float32)
    freqs = jnp.exp(index_f * (-2.0 * math.log(10000.0) / HEAD))
    angles = positions.astype(jnp.float32)[:, None] * freqs[None, :]
    return (jnp.tile(jnp.cos(angles), (1, 2 * heads)), jnp.tile(jnp.sin(angles), (1, 2 * heads)))


def total(value):
    for name in ("narrow", "wide"):
        size = lax.axis_size(name)
        if size & (size - 1):
            value = lax.psum(value, name)
            continue
        step = 1
        while step < size:
            value = value + lax.ppermute(value, name, [(d, d ^ step) for d in range(size)])
            step *= 2
    return value


def einsum(spec, left, right):
    return jnp.einsum(spec, left, right, preferred_element_type=jnp.float32)


def per_device(
    tokens,
    noise,
    seq_lengths,
    ln1_gain,
    ln1_bias,
    qkv_weight,
    out_weight,
    ln2_gain,
    ln2_bias,
    up_weight,
    up_bias,
    down_weight,
    down_bias,
    mask_vector,
    cotangent,
):
    f32 = jnp.float32
    bf16 = jnp.bfloat16
    both = ("narrow", "wide")
    ways = lax.axis_size("wide")
    parts = lax.axis_size("narrow")
    lane = lax.axis_index("wide")
    rows, width = tokens.shape
    group = rows * parts
    lw = qkv_weight.shape[2]
    ff = up_weight.shape[1]
    heads = lw // HEAD

    clean = tokens.astype(f32)
    normed1, norm1_pull = jax.vjp(layer_norm, clean, ln1_gain, ln1_bias)
    spot = mask_vector[None, :]
    normed_m, norm_m_pull = jax.vjp(layer_norm, spot, ln1_gain, ln1_bias)
    a_all = lax.all_gather(normed1.astype(bf16), "narrow", axis=0, tiled=True)
    noise_all = lax.all_gather(noise, "narrow", axis=0, tiled=True)
    spot_row = jnp.broadcast_to(normed_m.astype(bf16), (16, width))

    def share(weight):
        step = weight.shape[0] // ways
        return lax.dynamic_slice_in_dim(weight, lane * step, step, 0)

    a_all, up_s, down_s, out_s, bias_s = lax.optimization_barrier(
        (a_all, share(up_weight), share(down_weight), share(out_weight), up_bias)
    )
    out_full = lax.all_gather(out_s, both, axis=0, tiled=True)
    up_full = lax.all_gather(up_s, both, axis=0, tiled=True).reshape(parts, width, ff)
    down_full = lax.all_gather(down_s, both, axis=0, tiled=True).reshape(parts, ff, width)
    bias_full = lax.all_gather(bias_s, "narrow", axis=0)

    first, pos = token_meta(seq_lengths[0], group)
    cosines, sines = angle_tables(pos, heads)
    start = first[None, :].astype(jnp.int32)
    tile = min(TILE, group)
    tiles = group // tile
    at_head = first[::tile] // tile
    at_tail = (first[tile - 1 :: tile] + (tile - 1)) // tile
    span = jnp.stack([at_head, jnp.minimum(at_tail, jnp.arange(tiles))]).astype(jnp.int32)
    halves = qkv_weight[:2].reshape(2, width, heads, 2, HEAD // 2)
    wrot = jnp.stack([-halves[:, :, :, 1], halves[:, :, :, 0]], axis=3).reshape(2, width, lw)
    masked_all = noise_all[:, None]

    q, k, k_t, v, v_t = project(a_all, spot_row, masked_all, qkv_weight, wrot, cosines, sines)
    attn, lse = attend(span, q, k, v_t, start)

    sent = attn.reshape(2, parts, rows, lw)
    attn_rows = lax.all_to_all(sent, "narrow", 1, 1)
    attn_rows = attn_rows.transpose(0, 2, 1, 3).reshape(2, rows, width)
    masked = noise[:, None] == 1
    noisy = jnp.where(masked, spot, clean)
    resid = jnp.stack([noisy, clean])
    h_mid = resid + einsum("ctd,de->cte", attn_rows, out_full)
    normed2, norm2_pull = jax.vjp(layer_norm, h_mid, ln2_gain, ln2_bias)
    b = normed2.astype(bf16).reshape(2 * rows, width)
    up_pre = einsum("td,ndf->ntf", b, up_full) + bias_full[:, None, :]
    hidden_f, gelu_pull = jax.vjp(gelu_tanh, up_pre)
    hidden = hidden_f.astype(bf16)
    mlp_out = einsum("ntf,nfd->td", hidden, down_full).reshape(2, rows, width)
    output = (h_mid + mlp_out + down_bias).astype(bf16)

    cot = cotangent.reshape(2 * rows, width)
    grad_out = cotangent.astype(f32)
    d_down_bias = jnp.sum(grad_out, axis=(0, 1))
    d_hidden = einsum("td,nfd->ntf", cot, down_full)
    d_up_low = gelu_pull(d_hidden)[0].astype(bf16)
    d_b = einsum("ntf,ndf->td", d_up_low, up_full).reshape(2, rows, width)
    d_h_ln, d_ln2_gain, d_ln2_bias = norm2_pull(d_b)
    d_h_mid = grad_out + d_h_ln
    d_z = d_h_mid.astype(bf16)
    d_attn = einsum("cte,de->ctd", d_z, out_full).astype(bf16)
    d_attn = d_attn.reshape(2, rows, parts, lw).transpose(0, 2, 1, 3)
    d_attn = lax.all_to_all(d_attn, "narrow", 1, 1).reshape(2, group, lw)

    d_down = einsum("td,ntf->ndf", cot, hidden)
    d_up = einsum("td,ntf->ndf", b, d_up_low)
    d_up_bias = jnp.sum(d_up_low, axis=1, dtype=f32)
    d_out = einsum("cte,ctd->ed", d_z, attn_rows)
    d_out = d_out.reshape(width, parts, lw).transpose(1, 0, 2)

    def scatter(value):
        return lax.psum_scatter(
            value.astype(bf16).reshape(-1, value.shape[-1]), both, scatter_dimension=0, tiled=True
        ).astype(f32)

    d_down_mine = scatter(d_down).T
    d_up_mine = scatter(d_up)
    d_out_mine = scatter(d_out).T
    early = total(
        jnp.concatenate([d_ln2_gain, d_ln2_bias, d_down_bias, d_up_bias.reshape(-1)])
    )

    d_all, d_a_part, d_spot = attend_back(
        span, q, k, k_t, v, d_attn, attn, lse, start, masked_all, cosines, sines, qkv_weight
    )
    d_a = lax.psum_scatter(d_a_part, "narrow", scatter_dimension=0, tiled=True).astype(f32)
    d_spot = jnp.sum(d_spot, axis=1)
    d_qkv = einsum("td,xte->xde", a_all, d_all) + (
        spot_row[0].astype(f32)[None, :, None] * d_spot[:, None, :]
    )
    d_qkv = lax.psum_scatter(d_qkv.astype(bf16), "wide", scatter_dimension=1, tiled=True).astype(f32)
    d_a_spot = jnp.einsum(
        "xe,xde->d", d_spot, qkv_weight.astype(f32), precision=lax.Precision.HIGHEST
    )
    d_h_spot = jnp.sum(jnp.where(masked, d_h_mid[0], 0.0), axis=0)
    d_row, d_ln1_gain, d_ln1_bias = norm1_pull(d_a)
    d_tokens = (d_h_mid[1] + jnp.where(masked, 0.0, d_h_mid[0]) + d_row).astype(bf16)
    late = total(jnp.concatenate([d_ln1_gain, d_ln1_bias, d_h_spot, d_a_spot]))
    d_ln1_gain, d_ln1_bias, d_h_spot, d_a_spot = late.reshape(4, width)
    d_mask, gain_m, bias_m = norm_m_pull(d_a_spot[None, :])
    d_ln2_gain, d_ln2_bias, d_down_bias = early[: 3 * width].reshape(3, width)
    step = ff // ways
    mine = (lax.axis_index("narrow") * ways + lane) * step
    return (
        output,
        d_tokens,
        d_ln1_gain + gain_m,
        d_ln1_bias + bias_m,
        d_qkv,
        d_out_mine,
        d_ln2_gain,
        d_ln2_bias,
        d_up_mine,
        lax.dynamic_slice_in_dim(early[3 * width :], mine, step, 0),
        d_down_mine,
        d_down_bias,
        d_h_spot + d_mask[0],
    )


def solution(mesh):
    placed = (
        P(("wide", "narrow"), None),
        P(("wide", "narrow")),
        P("wide", None),
        P(),
        P(),
        P(None, None, "narrow"),
        P("narrow", None),
        P(),
        P(),
        P(None, "narrow"),
        P("narrow"),
        P("narrow", None),
        P(),
        P(),
        P(None, ("wide", "narrow"), None),
    )
    return jax.shard_map(
        per_device,
        mesh=mesh,
        in_specs=placed,
        out_specs=(
            P(None, ("wide", "narrow"), None),
            P(("wide", "narrow"), None),
            P(),
            P(),
            P(None, "wide", "narrow"),
            P("narrow", "wide"),
            P(),
            P(),
            P("wide", "narrow"),
            P(("narrow", "wide")),
            P("narrow", "wide"),
            P(),
            P(),
        ),
        check_vma=False,
    )
```
